256 devices in a mesh: layer: 2 (over core), row: 8 (over z_hi, y), col: 16 (over x, z_lo).
Axes of the slice: x: 4, y: 4, z: 8 (z_hi: 2, z_lo: 4; z = z_hi * 4 + z_lo), core: 2. Of those that a mesh axis runs over, the one named last changes fastest.
Arguments:
- amplitudes: bfloat16 [512, 128, 128], P(('row', 'col')), may hold values from -6 to 6
- integrals: bfloat16 [32768, 128, 128], P(('layer', 'row', 'col')), may hold values from -0.1875 to 0.1875
- amp_index: int32 [4096, 48], P(('layer', 'row', 'col')), may hold values from 0 to 31
- left_index: int32 [4096, 48], P(('layer', 'row', 'col')), may hold values from 0 to 127, as said below
- right_index: int32 [4096, 48], P(('layer', 'row', 'col')), may hold values from 0 to 127, as said below
- dest_col: int32 [2048, 1], P(('row', 'col')), may hold values from 0 to 15; in each aligned block of 16 rows (0 to 15, 16 to 31, ...) at most 2 rows name the same one
- owner_slot: int32 [2048], P(('row', 'col')), may hold values from 0 to 7
Outputs:
- ladder: float32 [1024, 128, 128], P(('row', 'col'))
The draws below stay inside these ranges and needn't reach their ends.
Inputs may be any that keep to these rules, and one draw needn't show every extreme that they name: `dest_col`: among the 16 result tiles of one index of row and col, no owner column appears more than 2 times, and some column appears exactly 2 times. A term's amplitude tile is number amp_index among the tiles of the devices with the same col index, counted row by row. A term's left and right integral tiles belong to one auxiliary function: left_index // 2 == right_index // 2. right_index // 2 == left_index // 2 for every term.
All inputs are finite; a program needn't handle non-finite values.
Results may differ from the reference program's by a relative error of at most 0.0029.
Values may be sent and summed in bfloat16 or wider, within the bound.
A program may use at most 64 MiB of HBM per device.

```python
import math
import jax
import jax.numpy as jnp
import numpy as np
from jax import lax

TILE = 128
AMP_DEV = 4
INTEGRAL_PER_GPU = 128
LOCAL = 16
TPR = 48
OWN = 8
CAP = 2
AMPLITUDE_COUNT = 512
INT_TILES = 32768
TASK_ROWS = 4096
SLOTS = 2048
N_LAYER = 2
N_ROW = 8
N_COL = 16


def term_tiles(key):
    base = jax.random.fold_in(key, 7331)
    aux_key = jax.random.fold_in(base, 1)
    side_key = jax.random.fold_in(base, 2)
    auxiliary = jax.random.randint(aux_key, (TASK_ROWS, TPR), 0, INTEGRAL_PER_GPU // 2, dtype=jnp.int32)
    sides = jax.random.randint(side_key, (2, TASK_ROWS, TPR), 0, 2, dtype=jnp.int32)
    left_tile_blocks = (2 * auxiliary + sides[0]).astype(jnp.int32)
    right_tiles = (2 * auxiliary + sides[1]).astype(jnp.int32)
    return (left_tile_blocks, right_tiles)


def draw_left_index(key, part):
    return term_tiles(key)[0]


def draw_right_index(key, part):
    return term_tiles(key)[1]


def plant(drawn, own_key, least, largest):
    spot = [jax.random.randint(jax.random.fold_in(own_key, axis), (), 0, length) for axis, length in enumerate(drawn.shape)]
    widest = drawn.shape.index(max(drawn.shape))
    next_to = spot[:widest] + [(spot[widest] + 1) % drawn.shape[widest]] + spot[widest + 1:]
    return drawn.at[tuple(spot)].set(least).at[tuple(next_to)].set(largest)


def level_of(stream_key, shape, shards, least, top_value):
    factor_of = 1.0
    for axis_at, parts in shards:
        heights = jax.random.uniform(jax.random.fold_in(jax.random.fold_in(stream_key, 6), axis_at), (parts,), jnp.float32, least / len(shards), top_value / len(shards))
        factor_of = factor_of * jnp.repeat(jnp.exp(heights), shape[axis_at] // parts).reshape((-1,) + (1,) * (len(shape) - 1 - axis_at))
    return factor_of


def deal_out(key, own, number, rows, count, top, reach, skew):
    ranking = jax.random.permutation(key, count)
    heavy_load, common = shares(count, rows * top, reach, skew, True), shares(count, rows * top, reach, skew, False)
    places = jnp.arange(count)

    def named(sizes, offset_by):
        used = int((sizes > 0).sum())
        fixed = max(1, used // 4)
        moved = fixed + (places - fixed + offset_by * (used - fixed)) % max(1, count - fixed)
        return jnp.zeros((count,), jnp.int32).at[ranking[jnp.where(places < fixed, places, moved)]].set(jnp.asarray(sizes, jnp.int32))

    sizes = jnp.where(number % 4 == 0, named(heavy_load, number // 4), named(common, number - number // 4 - 1))
    mixed = jax.random.permutation(jax.random.fold_in(own, 3), count)
    donor, taker = mixed[0:count // 2 * 2:2], mixed[1:count // 2 * 2:2]
    margin = jnp.minimum(sizes[donor] - 1, reach - sizes[taker]) // 2
    margin = jnp.where((donor == ranking[0]) | (taker == ranking[0]) | (sizes[taker] == 0), 0, jnp.maximum(margin, 0))
    moved = jax.random.randint(jax.random.fold_in(own, 4), (count // 2,), 0, 1 << 20) % (margin + 1)
    sizes = sizes.at[donor].add(-moved).at[taker].add(moved)
    members = jnp.searchsorted(jnp.cumsum(sizes), jnp.arange(rows * top), side="right").astype(jnp.int32)
    table = members.reshape(top, rows).T
    table = table[jax.random.permutation(jax.random.fold_in(own, 1), rows)]
    offset_by = jax.random.randint(jax.random.fold_in(own, 2), (rows, 1), 0, top)
    return jnp.take_along_axis(table, (jnp.arange(top)[None, :] + offset_by) % top, axis=1)


def shares(count, total, reach, lean, full):
    loads = [(1 << 20) // math.isqrt(rank ** lean) + 1 for rank in range(1, count + 1)]
    largest = reach if full else min(reach, max(-(-total // count), total * loads[0] // sum(loads)))
    least = 1 if total - largest >= count - 1 else 0
    given, spare = [largest] + [least] * (count - 1), total - largest - least * (count - 1)
    while spare > 0:
        candidates = [i for i in range(1, count) if given[i] < largest] or [i for i in range(1, count) if given[i] < reach]
        whole, remaining = sum([loads[i] for i in candidates]), spare
        for i in candidates:
            extra = min(reach - given[i], max(1, remaining * loads[i] // whole), spare)
            given[i] = given[i] + extra
            spare = spare - extra
    return np.array(given)


def bell_draw(rng, dims, deviation, reach, shards=(), kind=jnp.bfloat16):
    drawn = jax.random.normal(rng, dims, jnp.float32) * deviation
    if len(shards) > 0:
        drawn = level_of(rng, dims, shards, -0.22, 0.18) * drawn
    return jnp.clip(drawn, min=-reach, max=reach).astype(kind)


def setup_inputs(seed: int = 0) -> dict:
    seeds = jax.random.split(jax.random.key(seed), 8)
    amplitudes = bell_draw(seeds[0], (AMPLITUDE_COUNT, TILE, TILE), 1.0, 6.0, ((0, 128),))
    integrals = bell_draw(seeds[1], (INT_TILES, TILE, TILE), (8 * TILE) ** -0.5, 0.1875, ((0, 256),))
    amp_index = plant(jax.random.randint(seeds[2], (TASK_ROWS, TPR), 0, N_ROW * AMP_DEV), jax.random.fold_in(seeds[2], 1), 0, (N_ROW * AMP_DEV) - 1).astype(jnp.int32)
    left_index = draw_left_index(jax.random.fold_in(seeds[7], 71), 0)
    right_index = draw_right_index(jax.random.fold_in(seeds[7], 71), 0)
    dest_col_keys = jax.random.split(jax.random.fold_in(seeds[5], 1), SLOTS // LOCAL)
    dest_col_turns = jax.random.permutation(jax.random.fold_in(seeds[5], 3), SLOTS // LOCAL)
    dest_col = jax.vmap(lambda own, number: deal_out(jax.random.fold_in(seeds[5], 2), own, number, LOCAL, N_COL, 1, CAP, 2))(dest_col_keys, dest_col_turns).reshape((SLOTS, 1))
    owner_slot = plant(jax.random.randint(seeds[6], (SLOTS,), 0, OWN), jax.random.fold_in(seeds[6], 1), 0, OWN - 1).astype(jnp.int32)
    return dict(amplitudes=amplitudes, integrals=integrals, amp_index=amp_index, left_index=left_index, right_index=right_index, dest_col=dest_col, owner_slot=owner_slot)


def reference(amplitudes, integrals, amp_index, left_index, right_index, dest_col, owner_slot):
    groups = N_LAYER * N_ROW * N_COL

    def single_group(group):
        column = group % N_COL
        tiles = lax.dynamic_slice_in_dim(integrals, (group * INTEGRAL_PER_GPU).astype(jnp.int32), INTEGRAL_PER_GPU, 0)
        amp_rows = lax.dynamic_slice_in_dim(amp_index, (group * LOCAL).astype(jnp.int32), LOCAL, 0)
        left_rows = lax.dynamic_slice_in_dim(left_index, (group * LOCAL).astype(jnp.int32), LOCAL, 0)
        right_row_block = lax.dynamic_slice_in_dim(right_index, (group * LOCAL).astype(jnp.int32), LOCAL, 0)
        global_rows = (((amp_rows // AMP_DEV) * N_COL + column) * AMP_DEV + amp_rows % AMP_DEV).astype(jnp.int32)

        def one_slot(operand_list):
            amp_ids, left_ids, right_ids = operand_list
            amp_tiles = jnp.take(amplitudes, amp_ids, axis=0).astype(jnp.float32)
            right_tiles = jnp.take(tiles, right_ids, axis=0).astype(jnp.float32)
            middle_product = jnp.einsum('tcd,ted->tce', amp_tiles, right_tiles).astype(jnp.bfloat16)
            left_tile_blocks = jnp.take(tiles, left_ids, axis=0).astype(jnp.float32)
            return jnp.einsum('dov,dvh->oh', left_tile_blocks, middle_product.astype(jnp.float32))

        return lax.map(one_slot, (global_rows, left_rows, right_row_block))

    partials = lax.map(single_group, jnp.arange(groups, dtype=jnp.int32))
    partials = partials.reshape(N_LAYER, N_ROW * N_COL * LOCAL, TILE, TILE)
    slot_ids = jnp.arange(N_ROW * N_COL * LOCAL, dtype=jnp.int32)
    grid_row = slot_ids // (N_COL * LOCAL)
    target = ((grid_row * N_COL + dest_col[:, 0]) * OWN + owner_slot).astype(jnp.int32)
    ladder = jnp.zeros((N_ROW * N_COL * OWN, TILE, TILE), jnp.float32)
    for layer_id in range(N_LAYER):
        ladder = ladder.at[target].add(partials[layer_id])
    return ladder
```

```python
import jax
import jax.numpy as jnp
from jax import lax
from jax.experimental import pallas as pl
from jax.experimental.pallas import tpu as pltpu
from jax.sharding import PartitionSpec as P

MESH = pl.DeviceIdType.MESH
OWN = 8
AMP = 4
X, Y, ZLO = 4, 4, 4
COLS = X * ZLO
EARLY = COLS // 2
CHUNKS = 4


def product(left, right):
    return jnp.dot(left, right, preferred_element_type=jnp.float32)


def flip(bit):
    return 1 - bit


def other_half(row, far):
    return lax.rem(row + far * Y, 2 * Y)


def next_y(row, step):
    return (row // Y) * Y + lax.rem(row + step, Y)


def destination(col, place):
    x, z = col // ZLO, col % ZLO
    half, swap, dx = flip(place // EARLY), (place % EARLY) // X, place % X
    z = lax.rem(z + 2 * half, ZLO)
    z = z + swap * (1 - 2 * (z % 2))
    return lax.rem(x + dx, X) * ZLO + z


def kernel(amp_ix, left_ix, right_ix, dest, slot, amp_hbm, int_hbm, out,
           amps, ints, turned, part, stage_s, stage_i, got_s, got_i, got_f, tags, tags_in,
           order, first, count,
           local_sem, y_send, y_recv, z_send, z_recv, zy_send, zy_recv, f_send, f_recv,
           s_send, s_recv, i_send, i_recv, b_send, b_recv, t_send, t_recv):
    layer, row, col = lax.axis_index("layer"), lax.axis_index("row"), lax.axis_index("col")
    slots, terms = amp_ix.shape
    tiles = int_hbm.shape[0]
    edge = int_hbm.shape[1]
    half = AMP // 2
    mine = half * layer
    mate = {"layer": flip(layer)}
    far = other_half(row, 1)

    barrier = pltpu.get_barrier_semaphore()
    peers = [mate, {"row": far}]
    peers += [{"row": next_y(row, s)} for s in range(1, Y)]
    for peer in peers:
        pl.semaphore_signal(barrier, inc=1, device_id=peer, device_id_type=MESH)
    for place in range(COLS):
        if place != EARLY:
            pl.semaphore_signal(barrier, inc=1, device_id={"col": destination(col, place)}, device_id_type=MESH)

    own_amp = pltpu.make_async_copy(amp_hbm, amps.at[pl.ds(row * AMP, AMP)], local_sem.at[CHUNKS])
    own_amp.start()
    loads = []
    step = tiles // CHUNKS
    for c in range(CHUNKS):
        loads.append(pltpu.make_async_copy(int_hbm.at[pl.ds(c * step, step)], ints.at[pl.ds(c * step, step)], local_sem.at[c]))
        loads[-1].start()

    x, z = col // ZLO, col % ZLO

    def place_of(k):
        to = dest[k, 0]
        dx = lax.rem(to // ZLO - x + X, X)
        zt = lax.rem(to, ZLO)
        same = jnp.where(zt // 2 == z // 2, 1, 0)
        swap = jnp.where(zt % 2 == z % 2, 0, 1)
        return same * EARLY + swap * X + dx

    places = [place_of(k) for k in range(slots)]
    ranks = []
    for k in range(slots):
        rank = 0
        for j in range(slots):
            if j < k:
                rank = rank + jnp.where(places[j] <= places[k], 1, 0)
            elif j > k:
                rank = rank + jnp.where(places[j] < places[k], 1, 0)
        ranks.append(rank)
    for i in range(slots):
        at, below, same = 0, 0, 0
        for k in range(slots):
            at = at + jnp.where(ranks[k] == i, k, 0)
            below = below + jnp.where(places[k] < i, 1, 0)
            same = same + jnp.where(places[k] == i, 1, 0)
        order[i] = at
        first[i] = below
        count[i] = same

    def pick(place, j):
        at = jnp.minimum(first[place] + j, slots - 1)
        return at, j < count[place]

    def tag(place, _):
        for j in range(2):
            at, there = pick(place, j)
            tags[place, j] = jnp.full((8, edge), jnp.where(there, slot[order[at]], OWN), jnp.int32)
        return 0

    lax.fori_loop(0, COLS, tag, 0)

    def turn(c):
        loads[c].wait()

        def four(i, _):
            for j in range(4):
                turned[c * step + 4 * i + j] = ints[c * step + 4 * i + j].T
            return 0

        lax.fori_loop(0, step // 4, four, 0)

    turn(0)
    own_amp.wait()
    pl.semaphore_wait(barrier, len(peers) + COLS - 1)

    def block(r, n=half, at=0):
        return amps.at[pl.ds(r * AMP + mine + at, n)]

    def send(src, dst, out_sem, in_sem, peer):
        return pltpu.make_async_remote_copy(
            src_ref=src, dst_ref=dst, send_sem=out_sem, recv_sem=in_sem, device_id=peer, device_id_type=MESH
        )

    z_copies = [send(block(row, 1, t), block(row, 1, t), z_send.at[t], z_recv.at[t], {"row": far}) for t in range(half)]
    for c in z_copies:
        c.start()
    y_copies = [
        send(block(row), block(row), y_send.at[s - 1], y_recv.at[s - 1], {"row": next_y(row, s)}) for s in (1, 3, 2)
    ]
    for c in y_copies:
        c.start()
    tag_copies = []
    for place in range(COLS):
        if place != EARLY:
            tag_copies.append(send(tags.at[place], tags_in.at[place], t_send.at[place], t_recv.at[place],
                                   {"col": destination(col, place)}))
            tag_copies[-1].start()
    for c in range(1, CHUNKS):
        turn(c)

    to_mate = []

    def forward(r, n, at, k):
        to_mate.append(send(block(r, n, at), block(r, n, at), f_send.at[k], f_recv.at[k], mate))
        to_mate[-1].start()

    def arrived(r, n, at, sem):
        send(block(r, n, at), block(r, n, at), f_send.at[0], sem, mate).wait_recv()

    came = []
    k = 0
    for s in (1, 3, 2):
        r = next_y(row, Y - s)
        arrived(r, half, 0, y_recv.at[s - 1])
        forward(r, half, 0, k)
        came.append((r, half, 0, k))
        k += 1
    zy_copies = []
    for t in range(half):
        arrived(far, 1, t, z_recv.at[t])
        for s in (2, 1, 3):
            zy_copies.append(send(block(far, 1, t), block(far, 1, t), zy_send.at[t, s - 1], zy_recv.at[t, s - 1],
                                  {"row": next_y(row, s)}))
            zy_copies[-1].start()
        forward(far, 1, t, k)
        came.append((far, 1, t, k))
        k += 1
    for t in range(half):
        for s in (1, 3, 2):
            r = next_y(far, Y - s)
            arrived(r, 1, t, zy_recv.at[t, s - 1])
            forward(r, 1, t, k)
            came.append((r, 1, t, k))
            k += 1

    def of_mate(r, n, at):
        return amps.at[pl.ds(r * AMP + half * flip(layer) + at, n)]

    for r, n, at, k in came:
        send(of_mate(r, n, at), of_mate(r, n, at), f_send.at[0], f_recv.at[k], mate).wait_recv()
    for c in z_copies + y_copies + zy_copies + to_mate:
        c.wait_send()

    def s_copy(p):
        return send(stage_s.at[p], got_s.at[p], s_send.at[p], s_recv.at[p], mate)

    def i_copy(p):
        return send(stage_i.at[p], got_i.at[p], i_send.at[p], i_recv.at[p], {"col": destination(col, p)})

    def b_copy(p):
        return send(got_i.at[p], got_f.at[p], b_send.at[p], b_recv.at[p], mate)

    def chosen(p, j):
        at, there = pick(p, j)
        return part[at] * jnp.where(there, 1.0, 0.0)

    def to_sibling(p):
        stage_s[p] = chosen(p, flip(layer)).astype(jnp.bfloat16)
        s_copy(p).start()

    def both(p):
        s_copy(p).wait_recv()
        return (chosen(p, layer) + got_s[p].astype(jnp.float32)).astype(jnp.bfloat16)

    def to_owner(p):
        stage_i[p] = both(p)
        i_copy(p).start()

    def result(i):
        k = order[i]
        middles, lefts = [], []
        for t in range(terms):
            middles.append(product(amps[amp_ix[k, t]], turned[right_ix[k, t]]).astype(jnp.bfloat16))
            lefts.append(ints[left_ix[k, t]])
        part[i] = product(jnp.concatenate(lefts, 1), jnp.concatenate(middles, 0))

    def two(i, _):
        @pl.when(i >= 1)
        def _():
            to_sibling(i - 1)

        @pl.when(i >= 2)
        def _():
            to_owner(i - 2)

        result(2 * i)
        result(2 * i + 1)
        return 0

    lax.fori_loop(0, slots // 2, two, 0)

    def rest(p, _):
        to_sibling(p)
        return 0

    lax.fori_loop(EARLY - 1, COLS, rest, 0)
    to_owner(EARLY - 2)
    to_owner(EARLY - 1)
    got_i[EARLY] = both(EARLY)

    def rest_owner(p, _):
        to_owner(p)
        return 0

    lax.fori_loop(EARLY + 1, COLS, rest_owner, 0)
    b_copy(EARLY).start()

    def onward(p, _):
        i_copy(p).wait_recv()
        b_copy(p).start()
        return 0

    lax.fori_loop(0, EARLY, onward, 0)
    for place in range(COLS):
        if place != EARLY:
            send(tags.at[place], tags_in.at[place], t_send.at[place], t_recv.at[place], mate).wait_recv()
    tags_in[EARLY] = tags[EARLY]
    out[...] = jnp.zeros_like(out)

    def add(p, ref, j):
        label = tags_in[p, j]
        tile = ref[p].astype(jnp.float32).reshape(edge // 8, 8, edge)
        for s in range(OWN):
            there = jnp.where(label == s, 1.0, 0.0)
            out[s] += (tile * there[None]).reshape(edge, edge)

    def add_own(p, _):
        add(p, got_i, layer)
        return 0

    def add_mate(p, _):
        b_copy(p).wait_recv()
        add(p, got_f, flip(layer))
        return 0

    lax.fori_loop(0, EARLY + 1, add_own, 0)
    lax.fori_loop(0, EARLY + 1, add_mate, 0)

    lax.fori_loop(EARLY + 1, COLS, onward, 0)
    lax.fori_loop(EARLY + 1, COLS, add_own, 0)
    lax.fori_loop(EARLY + 1, COLS, add_mate, 0)

    def drain(p, _):
        s_copy(p).wait_send()
        b_copy(p).wait_send()
        return 0

    lax.fori_loop(0, COLS, drain, 0)
    for place in range(COLS):
        if place != EARLY:
            i_copy(place).wait_send()
    for c in tag_copies:
        c.wait_send()


def shards(amplitudes, integrals, amp_index, left_index, right_index, dest_col, owner_slot):
    edge = integrals.shape[1]
    half = AMP // 2
    rows = lax.axis_size("row")
    tile = (edge, edge)
    dma = pltpu.SemaphoreType.DMA
    in_smem = pl.BlockSpec(memory_space=pltpu.SMEM)
    in_hbm = pl.BlockSpec(memory_space=pl.ANY)
    forwards = 3 + half + 3 * half
    return pl.pallas_call(
        kernel,
        out_shape=jax.ShapeDtypeStruct((OWN, *tile), jnp.float32),
        in_specs=[in_smem] * 5 + [in_hbm] * 2,
        out_specs=pl.BlockSpec(memory_space=pltpu.VMEM),
        scratch_shapes=[
            pltpu.VMEM((rows * AMP, *tile), jnp.bfloat16),
            pltpu.VMEM(integrals.shape, jnp.bfloat16),
            pltpu.VMEM(integrals.shape, jnp.bfloat16),
            pltpu.VMEM((COLS, *tile), jnp.float32),
            pltpu.VMEM((COLS, *tile), jnp.bfloat16),
            pltpu.VMEM((COLS, *tile), jnp.bfloat16),
            pltpu.VMEM((COLS, *tile), jnp.bfloat16),
            pltpu.VMEM((COLS, *tile), jnp.bfloat16),
            pltpu.VMEM((COLS, *tile), jnp.bfloat16),
            pltpu.VMEM((COLS, 2, 8, edge), jnp.int32),
            pltpu.VMEM((COLS, 2, 8, edge), jnp.int32),
            pltpu.SMEM((COLS,), jnp.int32),
            pltpu.SMEM((COLS,), jnp.int32),
            pltpu.SMEM((COLS,), jnp.int32),
            dma((CHUNKS + 1,)),
            dma((3,)), dma((3,)),
            dma((half,)), dma((half,)),
            dma((half, 3)), dma((half, 3)),
            dma((forwards,)), dma((forwards,)),
            dma((COLS,)), dma((COLS,)),
            dma((COLS,)), dma((COLS,)),
            dma((COLS,)), dma((COLS,)),
            dma((COLS,)), dma((COLS,)),
        ],
        compiler_params=pltpu.CompilerParams(collective_id=0, has_side_effects=True),
    )(amp_index, left_index, right_index, dest_col, owner_slot, amplitudes, integrals)


def solution(mesh):
    placed = (
        P(("row", "col"), None, None),
        P(("layer", "row", "col"), None, None),
        P(("layer", "row", "col"), None),
        P(("layer", "row", "col"), None),
        P(("layer", "row", "col"), None),
        P(("row", "col"), None),
        P(("row", "col")),
    )
    return jax.shard_map(
        shards, mesh=mesh, in_specs=placed, out_specs=P(("row", "col"), None, None), check_vma=False
    )
```

```python
import jax
import jax.numpy as jnp
from jax import lax
from jax.experimental import pallas as pl
from jax.experimental.pallas import tpu as pltpu
from jax.sharding import PartitionSpec as P

MESH = pl.DeviceIdType.MESH
OWN = 8
AMP = 4
X, Y, ZLO = 4, 4, 4
COLS = X * ZLO
EARLY = COLS // 2
SELF = COLS - 1
CHUNKS = 4


def product(left, right):
    return jnp.dot(left, right, preferred_element_type=jnp.float32)


def flip(bit):
    return 1 - bit


def other_half(row, far):
    return lax.rem(row + far * Y, 2 * Y)


def next_y(row, step):
    return (row // Y) * Y + lax.rem(row + step, Y)


def destination(col, place):
    x, z = col // ZLO, col % ZLO
    half, swap, dx = flip(place // EARLY), flip((place % EARLY) // X), (place + 1) % X
    z = lax.rem(z + 2 * half, ZLO)
    z = z + swap * (1 - 2 * (z % 2))
    return lax.rem(x + dx, X) * ZLO + z


def kernel(amp_in, left_in, right_in, dest_in, slot_in, amp_hbm, int_hbm, result_ref,
           amp_ix, left_ix, right_ix, dest, slot, amps, ints, turned, part, stage_s, stage_i, got_s, got_i, got_f, tags, tags_in,
           order, first, count,
           local_sem, y_send, y_recv, z_send, z_recv, zy_send, zy_recv, f_send, f_recv,
           s_send, s_recv, i_send, i_recv, b_send, b_recv, t_send, t_recv, out, out_sem):
    layer, row, col = lax.axis_index("layer"), lax.axis_index("row"), lax.axis_index("col")
    slots, terms = amp_ix.shape
    tiles = int_hbm.shape[0]
    edge = int_hbm.shape[1]
    half = AMP // 2
    mine = half * layer
    mate = {"layer": flip(layer)}
    far = other_half(row, 1)

    barrier = pltpu.get_barrier_semaphore()
    peers = [mate, {"row": far}]
    peers += [{"row": next_y(row, s)} for s in range(1, Y)]
    for peer in peers:
        pl.semaphore_signal(barrier, inc=1, device_id=peer, device_id_type=MESH)
    for place in range(COLS):
        if place != SELF:
            pl.semaphore_signal(barrier, inc=1, device_id={"col": destination(col, place)}, device_id_type=MESH)

    own_amp = pltpu.make_async_copy(amp_hbm, amps.at[pl.ds(row * AMP, AMP)], local_sem.at[CHUNKS])
    own_amp.start()
    tables = []
    for n, (src, dst) in enumerate(
        ((dest_in, dest), (slot_in, slot), (amp_in, amp_ix), (left_in, left_ix), (right_in, right_ix))
    ):
        tables.append(pltpu.make_async_copy(src, dst, local_sem.at[CHUNKS + 1 + n]))
        tables[-1].start()
    loads = []
    step = tiles // CHUNKS
    for c in range(CHUNKS):
        loads.append(pltpu.make_async_copy(int_hbm.at[pl.ds(c * step, step)], ints.at[pl.ds(c * step, step)], local_sem.at[c]))
        loads[-1].start()

    def turn(c):
        loads[c].wait()

        def four(i, _):
            for j in range(4):
                turned[c * step + 4 * i + j] = ints[c * step + 4 * i + j].T
            return 0

        lax.fori_loop(0, step // 4, four, 0)

    turn(0)
    own_amp.wait()
    pl.semaphore_wait(barrier, len(peers) + COLS - 1)

    def block(r, n=half, at=0):
        return amps.at[pl.ds(r * AMP + mine + at, n)]

    def send(src, dst, out_sem, in_sem, peer):
        return pltpu.make_async_remote_copy(
            src_ref=src, dst_ref=dst, send_sem=out_sem, recv_sem=in_sem, device_id=peer, device_id_type=MESH
        )

    z_copies = [send(block(row, 1, t), block(row, 1, t), z_send.at[t], z_recv.at[t], {"row": far}) for t in range(half)]
    for c in z_copies:
        c.start()
    y_copies = [
        send(block(row), block(row), y_send.at[s - 1], y_recv.at[s - 1], {"row": next_y(row, s)}) for s in (1, 3, 2)
    ]
    for c in y_copies:
        c.start()
    x, z = col // ZLO, col % ZLO

    def place_of(k):
        to = dest[k]
        dx = lax.rem(to // ZLO - x + 2 * X - 1, X)
        zt = lax.rem(to, ZLO)
        same = jnp.where(zt // 2 == z // 2, 1, 0)
        even = jnp.where(zt % 2 == z % 2, 1, 0)
        return same * EARLY + even * X + dx

    for c in tables:
        c.wait()
    places = [place_of(k) for k in range(slots)]
    ranks = []
    for k in range(slots):
        rank = 0
        for j in range(slots):
            if j < k:
                rank = rank + jnp.where(places[j] <= places[k], 1, 0)
            elif j > k:
                rank = rank + jnp.where(places[j] < places[k], 1, 0)
        ranks.append(rank)
    for i in range(slots):
        at, below, same = 0, 0, 0
        for k in range(slots):
            at = at + jnp.where(ranks[k] == i, k, 0)
            below = below + jnp.where(places[k] < i, 1, 0)
            same = same + jnp.where(places[k] == i, 1, 0)
        order[i] = at
        first[i] = below
        count[i] = same

    turn(1)
    to_mate = []

    def forward(r, n, at, k):
        to_mate.append(send(block(r, n, at), block(r, n, at), f_send.at[k], f_recv.at[k], mate))
        to_mate[-1].start()

    def arrived(r, n, at, sem):
        send(block(r, n, at), block(r, n, at), f_send.at[0], sem, mate).wait_recv()

    came = []

    def take(r, n, at, sem):
        arrived(r, n, at, sem)
        forward(r, n, at, len(came))
        came.append((r, n, at, len(came)))

    zy_copies = []
    for t in range(half):
        arrived(far, 1, t, z_recv.at[t])
        for s in (2, 1, 3):
            zy_copies.append(send(block(far, 1, t), block(far, 1, t), zy_send.at[t, s - 1], zy_recv.at[t, s - 1],
                                  {"row": next_y(row, s)}))
            zy_copies[-1].start()
        forward(far, 1, t, len(came))
        came.append((far, 1, t, len(came)))
    for s in (1, 3, 2):
        take(next_y(row, Y - s), half, 0, y_recv.at[s - 1])
    for c in range(2, CHUNKS):
        turn(c)

    def pick(place, j):
        at = jnp.minimum(first[place] + j, slots - 1)
        return at, j < count[place]

    def tag(place, _):
        for j in range(2):
            at, there = pick(place, j)
            tags[place, j] = jnp.full((8, edge), jnp.where(there, slot[order[at]], OWN), jnp.int32)
        return 0

    lax.fori_loop(0, COLS, tag, 0)

    tag_copies = []
    for place in range(COLS):
        if place != SELF:
            tag_copies.append(send(tags.at[place], tags_in.at[place], t_send.at[place], t_recv.at[place],
                                   {"col": destination(col, place)}))
            tag_copies[-1].start()

    for t in range(half):
        for s in (1, 3, 2):
            take(next_y(far, Y - s), 1, t, zy_recv.at[t, s - 1])

    def of_mate(r, n, at):
        return amps.at[pl.ds(r * AMP + half * flip(layer) + at, n)]

    for r, n, at, k in came:
        send(of_mate(r, n, at), of_mate(r, n, at), f_send.at[0], f_recv.at[k], mate).wait_recv()
    for c in z_copies + y_copies + zy_copies + to_mate:
        c.wait_send()

    def s_copy(p):
        return send(stage_s.at[p], got_s.at[p], s_send.at[p], s_recv.at[p], mate)

    def i_copy(p):
        return send(stage_i.at[p], got_i.at[p], i_send.at[p], i_recv.at[p], {"col": destination(col, p)})

    def b_copy(p):
        return send(got_i.at[p], got_f.at[p], b_send.at[p], b_recv.at[p], mate)

    def chosen(p, j):
        at, there = pick(p, j)
        return part[at] * jnp.where(there, 1.0, 0.0)

    def add_sibling(i):
        part[i] += got_s[i].astype(jnp.float32)

    def stage_owner(p):
        stage_i[p] = chosen(p, layer).astype(jnp.bfloat16)

    def to_owner(p):
        stage_owner(p)
        i_copy(p).start()

    def result(i):
        k = order[i]
        middles, lefts = [], []
        for t in range(terms):
            middles.append(product(amps[amp_ix[k, t]], turned[right_ix[k, t]]).astype(jnp.bfloat16))
            lefts.append(ints[left_ix[k, t]])
        part[i] = product(jnp.concatenate(lefts, 1), jnp.concatenate(middles, 0))

    def two(i):
        for k in (2 * i, 2 * i + 1):
            result(k)
        for k in (2 * i, 2 * i + 1):
            stage_s[k] = part[k].astype(jnp.bfloat16)

    def start_two(i):
        for k in (2 * i, 2 * i + 1):
            s_copy(k).start()

    def opening(i, _):
        two(i)
        start_two(i)
        return 0

    def steady(i, _):
        for k in (2 * i - 4, 2 * i - 3):
            s_copy(k).wait_recv()
        for k in (2 * i - 4, 2 * i - 3):
            add_sibling(k)
        stage_owner(i - 2)
        two(i)
        start_two(i)
        i_copy(i - 2).start()
        return 0

    lax.fori_loop(0, 2, opening, 0)
    lax.fori_loop(2, slots // 2, steady, 0)
    for k in (slots - 4, slots - 3):
        s_copy(k).wait_recv()
        add_sibling(k)
    to_owner(EARLY - 2)
    for k in (slots - 2, slots - 1):
        s_copy(k).wait_recv()
        add_sibling(k)
    to_owner(EARLY - 1)

    def rest(p, _):
        to_owner(p)
        return 0

    lax.fori_loop(EARLY, SELF, rest, 0)
    got_i[SELF] = chosen(SELF, layer).astype(jnp.bfloat16)
    b_copy(SELF).start()
    for place in range(COLS):
        if place != SELF:
            send(tags.at[place], tags_in.at[place], t_send.at[place], t_recv.at[place], mate).wait_recv()
    tags_in[SELF] = tags[SELF]

    def add(p, ref, j):
        label = tags_in[p, j]
        tile = ref[p].astype(jnp.float32).reshape(edge // 8, 8, edge)
        for s in range(OWN):
            there = jnp.where(label == s, 1.0, 0.0)
            out[s] += (tile * there[None]).reshape(edge, edge)

    def onward(p, _):
        i_copy(p).wait_recv()
        b_copy(p).start()
        return 0

    def onward_add(p, _):
        onward(p, 0)
        add(p, got_i, layer)
        return 0

    def add_own(p, _):
        add(p, got_i, layer)
        return 0

    def add_mate(p, _):
        b_copy(p).wait_recv()
        add(p, got_f, flip(layer))
        return 0

    lax.fori_loop(0, EARLY - 1, onward, 0)
    out[...] = jnp.zeros_like(out)
    add_own(SELF, 0)
    lax.fori_loop(0, EARLY - 1, add_own, 0)
    add_mate(SELF, 0)
    lax.fori_loop(0, EARLY - 1, add_mate, 0)
    lax.fori_loop(EARLY - 1, SELF, onward_add, 0)
    lax.fori_loop(EARLY - 1, SELF, add_mate, 0)

    final = pltpu.make_async_copy(out, result_ref, out_sem)
    final.start()

    def drain(p, _):
        s_copy(p).wait_send()
        b_copy(p).wait_send()
        return 0

    lax.fori_loop(0, COLS, drain, 0)
    for place in range(COLS):
        if place != SELF:
            i_copy(place).wait_send()
    for c in tag_copies:
        c.wait_send()
    final.wait()


def shards(amplitudes, integrals, amp_index, left_index, right_index, dest_col, owner_slot):
    edge = integrals.shape[1]
    half = AMP // 2
    rows = lax.axis_size("row")
    tile = (edge, edge)
    dma = pltpu.SemaphoreType.DMA
    in_hbm = pl.BlockSpec(memory_space=pl.ANY)
    forwards = 3 + half + 3 * half
    return pl.pallas_call(
        kernel,
        out_shape=jax.ShapeDtypeStruct((OWN, *tile), jnp.float32),
        in_specs=[in_hbm] * 7,
        out_specs=pl.BlockSpec(memory_space=pl.ANY),
        scratch_shapes=[
            pltpu.SMEM(amp_index.shape, jnp.int32),
            pltpu.SMEM(left_index.shape, jnp.int32),
            pltpu.SMEM(right_index.shape, jnp.int32),
            pltpu.SMEM((COLS,), jnp.int32),
            pltpu.SMEM((COLS,), jnp.int32),
            pltpu.VMEM((rows * AMP, *tile), jnp.bfloat16),
            pltpu.VMEM(integrals.shape, jnp.bfloat16),
            pltpu.VMEM(integrals.shape, jnp.bfloat16),
            pltpu.VMEM((COLS, *tile), jnp.float32),
            pltpu.VMEM((COLS, *tile), jnp.bfloat16),
            pltpu.VMEM((COLS, *tile), jnp.bfloat16),
            pltpu.VMEM((COLS, *tile), jnp.bfloat16),
            pltpu.VMEM((COLS, *tile), jnp.bfloat16),
            pltpu.VMEM((COLS, *tile), jnp.bfloat16),
            pltpu.VMEM((COLS, 2, 8, edge), jnp.int32),
            pltpu.VMEM((COLS, 2, 8, edge), jnp.int32),
            pltpu.SMEM((COLS,), jnp.int32),
            pltpu.SMEM((COLS,), jnp.int32),
            pltpu.SMEM((COLS,), jnp.int32),
            dma((CHUNKS + 6,)),
            dma((3,)), dma((3,)),
            dma((half,)), dma((half,)),
            dma((half, 3)), dma((half, 3)),
            dma((forwards,)), dma((forwards,)),
            dma((COLS,)), dma((COLS,)),
            dma((COLS,)), dma((COLS,)),
            dma((COLS,)), dma((COLS,)),
            dma((COLS,)), dma((COLS,)),
            pltpu.VMEM((OWN, *tile), jnp.float32), dma(()),
        ],
        compiler_params=pltpu.CompilerParams(collective_id=0, has_side_effects=True, vmem_limit_bytes=24 << 20),
    )(
        *(
            pltpu.with_memory_space_constraint(v, pltpu.HBM)
            for v in (amp_index, left_index, right_index, dest_col.reshape(-1), owner_slot, amplitudes, integrals)
        )
    )


def solution(mesh):
    placed = (
        P(("row", "col"), None, None),
        P(("layer", "row", "col"), None, None),
        P(("layer", "row", "col"), None),
        P(("layer", "row", "col"), None),
        P(("layer", "row", "col"), None),
        P(("row", "col"), None),
        P(("row", "col")),
    )
    return jax.shard_map(
        shards, mesh=mesh, in_specs=placed, out_specs=P(("row", "col"), None, None), check_vma=False
    )
```

```python
import jax
import jax.numpy as jnp
from jax import lax
from jax.experimental import pallas as pl
from jax.experimental.pallas import tpu as pltpu
from jax.sharding import PartitionSpec as P

MESH = pl.DeviceIdType.MESH
OWN = 8
AMP = 4
X, Y, ZLO = 4, 4, 4
COLS = X * ZLO
EARLY = COLS // 2
SELF = COLS - 1
CHUNKS = 4


def product(left, right):
    return jnp.dot(left, right, preferred_element_type=jnp.float32)


def flip(bit):
    return 1 - bit


def other_half(row, far):
    return lax.rem(row + far * Y, 2 * Y)


def next_y(row, step):
    return (row // Y) * Y + lax.rem(row + step, Y)


def destination(col, place):
    x, z = col // ZLO, col % ZLO
    half, swap, dx = flip(place // EARLY), flip((place % EARLY) // X), (place + 1) % X
    z = lax.rem(z + 2 * half, ZLO)
    z = z + swap * (1 - 2 * (z % 2))
    return lax.rem(x + dx, X) * ZLO + z


def kernel(amp_in, left_in, right_in, dest_in, slot_in, amp_hbm, int_hbm, result_ref,
           amp_ix, left_ix, right_ix, dest, slot, amps, ints, turned, part, stage_s, stage_i, got_s, got_i, got_f, tags, tags_in,
           order, first, count,
           local_sem, y_send, y_recv, z_send, z_recv, zy_send, zy_recv, f_send, f_recv,
           s_send, s_recv, i_send, i_recv, b_send, b_recv, t_send, t_recv, out, out_sem):
    layer, row, col = lax.axis_index("layer"), lax.axis_index("row"), lax.axis_index("col")
    slots, terms = amp_ix.shape
    tiles = int_hbm.shape[0]
    edge = int_hbm.shape[1]
    half = AMP // 2
    mine = half * layer
    mate = {"layer": flip(layer)}
    far = other_half(row, 1)

    barrier = pltpu.get_barrier_semaphore()
    peers = [mate, {"row": far}]
    peers += [{"row": next_y(row, s)} for s in range(1, Y)]
    for peer in peers:
        pl.semaphore_signal(barrier, inc=1, device_id=peer, device_id_type=MESH)
    for place in range(COLS):
        if place != SELF:
            pl.semaphore_signal(barrier, inc=1, device_id={"col": destination(col, place)}, device_id_type=MESH)

    own_amp = pltpu.make_async_copy(amp_hbm, amps.at[pl.ds(row * AMP, AMP)], local_sem.at[CHUNKS])
    own_amp.start()
    tables = []
    for n, (src, dst) in enumerate(
        ((dest_in, dest), (slot_in, slot), (amp_in, amp_ix), (left_in, left_ix), (right_in, right_ix))
    ):
        tables.append(pltpu.make_async_copy(src, dst, local_sem.at[CHUNKS + 1 + n]))
        tables[-1].start()
    loads = []
    step = tiles // CHUNKS
    for c in range(CHUNKS):
        loads.append(pltpu.make_async_copy(int_hbm.at[pl.ds(c * step, step)], ints.at[pl.ds(c * step, step)], local_sem.at[c]))
        loads[-1].start()

    def turn(c):
        loads[c].wait()

        def four(i, _):
            for j in range(4):
                turned[c * step + 4 * i + j] = ints[c * step + 4 * i + j].T
            return 0

        lax.fori_loop(0, step // 4, four, 0)

    turn(0)
    own_amp.wait()
    pl.semaphore_wait(barrier, len(peers) + COLS - 1)

    def block(r, n=half, at=0):
        return amps.at[pl.ds(r * AMP + mine + at, n)]

    def send(src, dst, out_sem, in_sem, peer):
        return pltpu.make_async_remote_copy(
            src_ref=src, dst_ref=dst, send_sem=out_sem, recv_sem=in_sem, device_id=peer, device_id_type=MESH
        )

    z_copies = [send(block(row, 1, t), block(row, 1, t), z_send.at[t], z_recv.at[t], {"row": far}) for t in range(half)]
    for c in z_copies:
        c.start()
    y_copies = [
        send(block(row), block(row), y_send.at[s - 1], y_recv.at[s - 1], {"row": next_y(row, s)}) for s in (1, 3, 2)
    ]
    for c in y_copies:
        c.start()
    x, z = col // ZLO, col % ZLO

    def place_of(k):
        to = dest[k]
        dx = lax.rem(to // ZLO - x + 2 * X - 1, X)
        zt = lax.rem(to, ZLO)
        same = jnp.where(zt // 2 == z // 2, 1, 0)
        even = jnp.where(zt % 2 == z % 2, 1, 0)
        return same * EARLY + even * X + dx

    for c in tables:
        c.wait()
    places = [place_of(k) for k in range(slots)]
    ranks = []
    for k in range(slots):
        rank = 0
        for j in range(slots):
            if j < k:
                rank = rank + jnp.where(places[j] <= places[k], 1, 0)
            elif j > k:
                rank = rank + jnp.where(places[j] < places[k], 1, 0)
        ranks.append(rank)
    for i in range(slots):
        at, below, same = 0, 0, 0
        for k in range(slots):
            at = at + jnp.where(ranks[k] == i, k, 0)
            below = below + jnp.where(places[k] < i, 1, 0)
            same = same + jnp.where(places[k] == i, 1, 0)
        order[i] = at
        first[i] = below
        count[i] = same

    turn(1)
    to_mate = []

    def forward(r, n, at, k):
        to_mate.append(send(block(r, n, at), block(r, n, at), f_send.at[k], f_recv.at[k], mate))
        to_mate[-1].start()

    def arrived(r, n, at, sem):
        send(block(r, n, at), block(r, n, at), f_send.at[0], sem, mate).wait_recv()

    came = []

    def take(r, n, at, sem):
        arrived(r, n, at, sem)
        forward(r, n, at, len(came))
        came.append((r, n, at, len(came)))

    zy_copies = []
    for t in range(half):
        arrived(far, 1, t, z_recv.at[t])
        for s in (2, 1, 3):
            zy_copies.append(send(block(far, 1, t), block(far, 1, t), zy_send.at[t, s - 1], zy_recv.at[t, s - 1],
                                  {"row": next_y(row, s)}))
            zy_copies[-1].start()
        forward(far, 1, t, len(came))
        came.append((far, 1, t, len(came)))
    for s in (1, 3, 2):
        take(next_y(row, Y - s), half, 0, y_recv.at[s - 1])
    for c in range(2, CHUNKS):
        turn(c)

    def pick(place, j):
        at = jnp.minimum(first[place] + j, slots - 1)
        return at, j < count[place]

    def tag(place, _):
        for j in range(2):
            at, there = pick(place, j)
            tags[place, j] = jnp.full((8, edge), jnp.where(there, slot[order[at]], OWN), jnp.int32)
        return 0

    lax.fori_loop(0, COLS, tag, 0)

    tag_copies = []
    for place in range(COLS):
        if place != SELF:
            tag_copies.append(send(tags.at[place], tags_in.at[place], t_send.at[place], t_recv.at[place],
                                   {"col": destination(col, place)}))
            tag_copies[-1].start()

    for t in range(half):
        for s in (1, 3, 2):
            take(next_y(far, Y - s), 1, t, zy_recv.at[t, s - 1])

    def of_mate(r, n, at):
        return amps.at[pl.ds(r * AMP + half * flip(layer) + at, n)]

    for r, n, at, k in came:
        send(of_mate(r, n, at), of_mate(r, n, at), f_send.at[0], f_recv.at[k], mate).wait_recv()
    for c in z_copies + y_copies + zy_copies + to_mate:
        c.wait_send()

    def s_copy(p):
        return send(stage_s.at[p], got_s.at[p], s_send.at[p], s_recv.at[p], mate)

    def i_copy(p):
        return send(stage_i.at[p], got_i.at[p], i_send.at[p], i_recv.at[p], {"col": destination(col, p)})

    def b_copy(p):
        return send(got_i.at[p], got_f.at[p], b_send.at[p], b_recv.at[p], mate)

    def chosen(p, j):
        at, there = pick(p, j)
        return part[at] * jnp.where(there, 1.0, 0.0)

    def add_sibling(i):
        part[i] += got_s[i].astype(jnp.float32)

    def stage_owner(p):
        stage_i[p] = chosen(p, layer).astype(jnp.bfloat16)

    def to_owner(p):
        stage_owner(p)
        i_copy(p).start()

    def result(i):
        k = order[i]
        middles, lefts = [], []
        for t in range(terms):
            middles.append(product(amps[amp_ix[k, t]], turned[right_ix[k, t]]).astype(jnp.bfloat16))
            lefts.append(ints[left_ix[k, t]])
        part[i] = product(jnp.concatenate(lefts, 1), jnp.concatenate(middles, 0))

    def two(i):
        for k in (2 * i, 2 * i + 1):
            result(k)
        for k in (2 * i, 2 * i + 1):
            stage_s[k] = part[k].astype(jnp.bfloat16)

    def start_two(i):
        for k in (2 * i, 2 * i + 1):
            s_copy(k).start()

    def opening(i, _):
        two(i)
        start_two(i)
        return 0

    def steady(i, _):
        for k in (2 * i - 4, 2 * i - 3):
            s_copy(k).wait_recv()
        for k in (2 * i - 4, 2 * i - 3):
            add_sibling(k)
        to_owner(i - 2)
        two(i)
        start_two(i)
        return 0

    lax.fori_loop(0, 2, opening, 0)
    lax.fori_loop(2, slots // 2, steady, 0)
    for k in (slots - 4, slots - 3):
        s_copy(k).wait_recv()
        add_sibling(k)
    to_owner(EARLY - 2)
    for k in (slots - 2, slots - 1):
        s_copy(k).wait_recv()
        add_sibling(k)
    to_owner(EARLY - 1)

    def rest(p, _):
        to_owner(p)
        return 0

    lax.fori_loop(EARLY, SELF, rest, 0)
    got_i[SELF] = chosen(SELF, layer).astype(jnp.bfloat16)
    b_copy(SELF).start()
    for place in range(COLS):
        if place != SELF:
            send(tags.at[place], tags_in.at[place], t_send.at[place], t_recv.at[place], mate).wait_recv()
    tags_in[SELF] = tags[SELF]

    def add(p, ref, j):
        label = tags_in[p, j]
        tile = ref[p].astype(jnp.float32).reshape(edge // 8, 8, edge)
        for s in range(OWN):
            there = jnp.where(label == s, 1.0, 0.0)
            out[s] += (tile * there[None]).reshape(edge, edge)

    def onward(p, _):
        i_copy(p).wait_recv()
        b_copy(p).start()
        return 0

    def onward_add(p, _):
        onward(p, 0)
        add(p, got_i, layer)
        return 0

    def add_own(p, _):
        add(p, got_i, layer)
        return 0

    def add_mate(p, _):
        b_copy(p).wait_recv()
        add(p, got_f, flip(layer))
        return 0

    lax.fori_loop(0, EARLY - 1, onward, 0)
    out[...] = jnp.zeros_like(out)
    add_own(SELF, 0)
    lax.fori_loop(0, EARLY - 1, add_own, 0)
    add_mate(SELF, 0)
    lax.fori_loop(0, EARLY - 1, add_mate, 0)
    lax.fori_loop(EARLY - 1, SELF, onward_add, 0)
    lax.fori_loop(EARLY - 1, SELF, add_mate, 0)

    final = pltpu.make_async_copy(out, result_ref, out_sem)
    final.start()

    def drain(p, _):
        s_copy(p).wait_send()
        b_copy(p).wait_send()
        return 0

    lax.fori_loop(0, COLS, drain, 0)
    for place in range(COLS):
        if place != SELF:
            i_copy(place).wait_send()
    for c in tag_copies:
        c.wait_send()
    final.wait()


def shards(amplitudes, integrals, amp_index, left_index, right_index, dest_col, owner_slot):
    edge = integrals.shape[1]
    half = AMP // 2
    rows = lax.axis_size("row")
    tile = (edge, edge)
    dma = pltpu.SemaphoreType.DMA
    in_hbm = pl.BlockSpec(memory_space=pl.ANY)
    forwards = 3 + half + 3 * half
    return pl.pallas_call(
        kernel,
        out_shape=jax.ShapeDtypeStruct((OWN, *tile), jnp.float32),
        in_specs=[in_hbm] * 7,
        out_specs=pl.BlockSpec(memory_space=pl.ANY),
        scratch_shapes=[
            pltpu.SMEM(amp_index.shape, jnp.int32),
            pltpu.SMEM(left_index.shape, jnp.int32),
            pltpu.SMEM(right_index.shape, jnp.int32),
            pltpu.SMEM((COLS,), jnp.int32),
            pltpu.SMEM((COLS,), jnp.int32),
            pltpu.VMEM((rows * AMP, *tile), jnp.bfloat16),
            pltpu.VMEM(integrals.shape, jnp.bfloat16),
            pltpu.VMEM(integrals.shape, jnp.bfloat16),
            pltpu.VMEM((COLS, *tile), jnp.float32),
            pltpu.VMEM((COLS, *tile), jnp.bfloat16),
            pltpu.VMEM((COLS, *tile), jnp.bfloat16),
            pltpu.VMEM((COLS, *tile), jnp.bfloat16),
            pltpu.VMEM((COLS, *tile), jnp.bfloat16),
            pltpu.VMEM((COLS, *tile), jnp.bfloat16),
            pltpu.VMEM((COLS, 2, 8, edge), jnp.int32),
            pltpu.VMEM((COLS, 2, 8, edge), jnp.int32),
            pltpu.SMEM((COLS,), jnp.int32),
            pltpu.SMEM((COLS,), jnp.int32),
            pltpu.SMEM((COLS,), jnp.int32),
            dma((CHUNKS + 6,)),
            dma((3,)), dma((3,)),
            dma((half,)), dma((half,)),
            dma((half, 3)), dma((half, 3)),
            dma((forwards,)), dma((forwards,)),
            dma((COLS,)), dma((COLS,)),
            dma((COLS,)), dma((COLS,)),
            dma((COLS,)), dma((COLS,)),
            dma((COLS,)), dma((COLS,)),
            pltpu.VMEM((OWN, *tile), jnp.float32), dma(()),
        ],
        compiler_params=pltpu.CompilerParams(collective_id=0, has_side_effects=True, vmem_limit_bytes=24 << 20),
    )(
        *(
            pltpu.with_memory_space_constraint(v, pltpu.HBM)
            for v in (amp_index, left_index, right_index, dest_col.reshape(-1), owner_slot, amplitudes, integrals)
        )
    )


def solution(mesh):
    placed = (
        P(("row", "col"), None, None),
        P(("layer", "row", "col"), None, None),
        P(("layer", "row", "col"), None),
        P(("layer", "row", "col"), None),
        P(("layer", "row", "col"), None),
        P(("row", "col"), None),
        P(("row", "col")),
    )
    return jax.shard_map(
        shards, mesh=mesh, in_specs=placed, out_specs=P(("row", "col"), None, None), check_vma=False
    )
```

```python
import jax
import jax.numpy as jnp
from jax import lax
from jax.experimental import pallas as pl
from jax.experimental.pallas import tpu as pltpu
from jax.sharding import PartitionSpec as P

MESH = pl.DeviceIdType.MESH
OWN = 8
AMP = 4
X, Y, ZLO = 4, 4, 4
COLS = X * ZLO
EARLY = COLS // 2
SELF = COLS - 1
CHUNKS = 4


def product(left, right):
    return jnp.dot(left, right, preferred_element_type=jnp.float32)


def flip(bit):
    return 1 - bit


def other_half(row, far):
    return lax.rem(row + far * Y, 2 * Y)


def next_y(row, step):
    return (row // Y) * Y + lax.rem(row + step, Y)


def destination(col, place):
    x, z = col // ZLO, col % ZLO
    half, swap, dx = flip(place // EARLY), flip((place % EARLY) // X), (place + 1) % X
    z = lax.rem(z + 2 * half, ZLO)
    z = z + swap * (1 - 2 * (z % 2))
    return lax.rem(x + dx, X) * ZLO + z


def kernel(amp_in, left_in, right_in, dest_in, slot_in, amp_hbm, int_hbm, result_ref,
           amp_ix, left_ix, right_ix, dest, slot, amps, ints, turned, part, stage_s, stage_i, got_s, got_i, got_f, tags, tags_in,
           order, first, count,
           local_sem, y_send, y_recv, z_send, z_recv, zy_send, zy_recv, f_send, f_recv,
           s_send, s_recv, i_send, i_recv, b_send, b_recv, t_send, t_recv, out, out_sem):
    layer, row, col = lax.axis_index("layer"), lax.axis_index("row"), lax.axis_index("col")
    slots, terms = amp_ix.shape
    tiles = int_hbm.shape[0]
    edge = int_hbm.shape[1]
    half = AMP // 2
    mine = half * layer
    mate = {"layer": flip(layer)}
    far = other_half(row, 1)

    barrier = pltpu.get_barrier_semaphore()
    peers = [mate, {"row": far}]
    peers += [{"row": next_y(row, s)} for s in range(1, Y)]
    for peer in peers:
        pl.semaphore_signal(barrier, inc=1, device_id=peer, device_id_type=MESH)
    for place in range(COLS):
        if place != SELF:
            pl.semaphore_signal(barrier, inc=1, device_id={"col": destination(col, place)}, device_id_type=MESH)

    own_amp = pltpu.make_async_copy(amp_hbm, amps.at[pl.ds(row * AMP, AMP)], local_sem.at[CHUNKS])
    own_amp.start()
    tables = []
    for n, (src, dst) in enumerate(
        ((dest_in, dest), (slot_in, slot), (amp_in, amp_ix), (left_in, left_ix), (right_in, right_ix))
    ):
        tables.append(pltpu.make_async_copy(src, dst, local_sem.at[CHUNKS + 1 + n]))
        tables[-1].start()
    loads = []
    step = tiles // CHUNKS
    for c in range(CHUNKS):
        loads.append(pltpu.make_async_copy(int_hbm.at[pl.ds(c * step, step)], ints.at[pl.ds(c * step, step)], local_sem.at[c]))
        loads[-1].start()

    def turn(c):
        loads[c].wait()

        def four(i, _):
            for j in range(4):
                turned[c * step + 4 * i + j] = ints[c * step + 4 * i + j].T
            return 0

        lax.fori_loop(0, step // 4, four, 0)

    turn(0)
    own_amp.wait()
    pl.semaphore_wait(barrier, len(peers) + COLS - 1)

    def block(r, n=half, at=0):
        return amps.at[pl.ds(r * AMP + mine + at, n)]

    def send(src, dst, out_sem, in_sem, peer):
        return pltpu.make_async_remote_copy(
            src_ref=src, dst_ref=dst, send_sem=out_sem, recv_sem=in_sem, device_id=peer, device_id_type=MESH
        )

    z_copies = [send(block(row, 1, t), block(row, 1, t), z_send.at[t], z_recv.at[t], {"row": far}) for t in range(half)]
    for c in z_copies:
        c.start()
    y_copies = [
        send(block(row), block(row), y_send.at[s - 1], y_recv.at[s - 1], {"row": next_y(row, s)}) for s in (1, 3, 2)
    ]
    for c in y_copies:
        c.start()
    x, z = col // ZLO, col % ZLO

    def place_of(k):
        to = dest[k]
        dx = lax.rem(to // ZLO - x + 2 * X - 1, X)
        zt = lax.rem(to, ZLO)
        same = jnp.where(zt // 2 == z // 2, 1, 0)
        even = jnp.where(zt % 2 == z % 2, 1, 0)
        return same * EARLY + even * X + dx

    for c in tables:
        c.wait()
    places = [place_of(k) for k in range(slots)]
    ranks = []
    for k in range(slots):
        rank = 0
        for j in range(slots):
            if j < k:
                rank = rank + jnp.where(places[j] <= places[k], 1, 0)
            elif j > k:
                rank = rank + jnp.where(places[j] < places[k], 1, 0)
        ranks.append(rank)
    for i in range(slots):
        at, below, same = 0, 0, 0
        for k in range(slots):
            at = at + jnp.where(ranks[k] == i, k, 0)
            below = below + jnp.where(places[k] < i, 1, 0)
            same = same + jnp.where(places[k] == i, 1, 0)
        order[i] = at
        first[i] = below
        count[i] = same

    turn(1)
    to_mate = []

    def forward(r, n, at, k):
        to_mate.append(send(block(r, n, at), block(r, n, at), f_send.at[k], f_recv.at[k], mate))
        to_mate[-1].start()

    def arrived(r, n, at, sem):
        send(block(r, n, at), block(r, n, at), f_send.at[0], sem, mate).wait_recv()

    came = []

    def take(r, n, at, sem):
        arrived(r, n, at, sem)
        forward(r, n, at, len(came))
        came.append((r, n, at, len(came)))

    zy_copies = []
    for t in range(half):
        arrived(far, 1, t, z_recv.at[t])
        for s in (2, 1, 3):
            zy_copies.append(send(block(far, 1, t), block(far, 1, t), zy_send.at[t, s - 1], zy_recv.at[t, s - 1],
                                  {"row": next_y(row, s)}))
            zy_copies[-1].start()
        forward(far, 1, t, len(came))
        came.append((far, 1, t, len(came)))
    for s in (1, 3, 2):
        take(next_y(row, Y - s), half, 0, y_recv.at[s - 1])
    for c in range(2, CHUNKS):
        turn(c)

    def pick(place, j):
        at = jnp.minimum(first[place] + j, slots - 1)
        return at, j < count[place]

    def tag(place, _):
        for j in range(2):
            at, there = pick(place, j)
            tags[place, j] = jnp.full((8, edge), jnp.where(there, slot[order[at]], OWN), jnp.int32)
        return 0

    lax.fori_loop(0, COLS, tag, 0)

    tag_copies = []
    for place in range(COLS):
        if place != SELF:
            tag_copies.append(send(tags.at[place], tags_in.at[place], t_send.at[place], t_recv.at[place],
                                   {"col": destination(col, place)}))
            tag_copies[-1].start()

    for t in range(half):
        for s in (1, 3, 2):
            take(next_y(far, Y - s), 1, t, zy_recv.at[t, s - 1])

    def of_mate(r, n, at):
        return amps.at[pl.ds(r * AMP + half * flip(layer) + at, n)]

    for r, n, at, k in came:
        send(of_mate(r, n, at), of_mate(r, n, at), f_send.at[0], f_recv.at[k], mate).wait_recv()

    def s_copy(p):
        return send(stage_s.at[p], got_s.at[p], s_send.at[p], s_recv.at[p], mate)

    def i_copy(p):
        return send(stage_i.at[p], got_i.at[p], i_send.at[p], i_recv.at[p], {"col": destination(col, p)})

    def b_copy(p):
        return send(got_i.at[p], got_f.at[p], b_send.at[p], b_recv.at[p], mate)

    def chosen(p, j):
        at, there = pick(p, j)
        return part[at] * jnp.where(there, 1.0, 0.0)

    def add_sibling(i):
        part[i] += got_s[i].astype(jnp.float32)

    def stage_owner(p):
        stage_i[p] = chosen(p, layer).astype(jnp.bfloat16)

    def to_owner(p):
        stage_owner(p)
        i_copy(p).start()

    def result(i):
        k = order[i]
        middles, lefts = [], []
        for t in range(terms):
            middles.append(product(amps[amp_ix[k, t]], turned[right_ix[k, t]]).astype(jnp.bfloat16))
            lefts.append(ints[left_ix[k, t]])
        part[i] = product(jnp.concatenate(lefts, 1), jnp.concatenate(middles, 0))

    def two(i):
        for k in (2 * i, 2 * i + 1):
            result(k)
        for k in (2 * i, 2 * i + 1):
            stage_s[k] = part[k].astype(jnp.bfloat16)

    def start_two(i):
        for k in (2 * i, 2 * i + 1):
            s_copy(k).start()

    def opening(i, _):
        two(i)
        start_two(i)
        return 0

    def steady(i, _):
        for k in (2 * i - 4, 2 * i - 3):
            s_copy(k).wait_recv()
        for k in (2 * i - 4, 2 * i - 3):
            add_sibling(k)
        to_owner(i - 2)
        two(i)
        start_two(i)
        return 0

    lax.fori_loop(0, 2, opening, 0)
    lax.fori_loop(2, slots // 2, steady, 0)
    for k in (slots - 4, slots - 3):
        s_copy(k).wait_recv()
        add_sibling(k)
    to_owner(EARLY - 2)
    for k in (slots - 2, slots - 1):
        s_copy(k).wait_recv()
        add_sibling(k)
    to_owner(EARLY - 1)

    def rest(p, _):
        to_owner(p)
        return 0

    lax.fori_loop(EARLY, SELF, rest, 0)
    got_i[SELF] = chosen(SELF, layer).astype(jnp.bfloat16)
    b_copy(SELF).start()
    for place in range(COLS):
        if place != SELF:
            send(tags.at[place], tags_in.at[place], t_send.at[place], t_recv.at[place], mate).wait_recv()
    tags_in[SELF] = tags[SELF]

    def add(p, ref, j):
        label = tags_in[p, j]
        tile = ref[p].astype(jnp.float32).reshape(edge // 8, 8, edge)
        for s in range(OWN):
            there = jnp.where(label == s, 1.0, 0.0)
            out[s] += (tile * there[None]).reshape(edge, edge)

    def onward(p, _):
        i_copy(p).wait_recv()
        b_copy(p).start()
        return 0

    def onward_add(p, _):
        onward(p, 0)
        add(p, got_i, layer)
        return 0

    def add_own(p, _):
        add(p, got_i, layer)
        return 0

    def add_mate(p, _):
        b_copy(p).wait_recv()
        add(p, got_f, flip(layer))
        return 0

    lax.fori_loop(0, EARLY - 1, onward, 0)
    out[...] = jnp.zeros_like(out)
    add_own(SELF, 0)
    lax.fori_loop(0, EARLY - 1, add_own, 0)
    add_mate(SELF, 0)
    lax.fori_loop(0, EARLY - 1, add_mate, 0)
    lax.fori_loop(EARLY - 1, SELF, onward_add, 0)
    lax.fori_loop(EARLY - 1, SELF, add_mate, 0)

    final = pltpu.make_async_copy(out, result_ref, out_sem)
    final.start()

    def drain(p, _):
        s_copy(p).wait_send()
        b_copy(p).wait_send()
        return 0

    lax.fori_loop(0, COLS, drain, 0)
    for c in z_copies + y_copies + zy_copies + to_mate:
        c.wait_send()
    for place in range(COLS):
        if place != SELF:
            i_copy(place).wait_send()
    for c in tag_copies:
        c.wait_send()
    final.wait()


def shards(amplitudes, integrals, amp_index, left_index, right_index, dest_col, owner_slot):
    edge = integrals.shape[1]
    half = AMP // 2
    rows = lax.axis_size("row")
    tile = (edge, edge)
    dma = pltpu.SemaphoreType.DMA
    in_hbm = pl.BlockSpec(memory_space=pl.ANY)
    forwards = 3 + half + 3 * half
    return pl.pallas_call(
        kernel,
        out_shape=jax.ShapeDtypeStruct((OWN, *tile), jnp.float32),
        in_specs=[in_hbm] * 7,
        out_specs=pl.BlockSpec(memory_space=pl.ANY),
        scratch_shapes=[
            pltpu.SMEM(amp_index.shape, jnp.int32),
            pltpu.SMEM(left_index.shape, jnp.int32),
            pltpu.SMEM(right_index.shape, jnp.int32),
            pltpu.SMEM((COLS,), jnp.int32),
            pltpu.SMEM((COLS,), jnp.int32),
            pltpu.VMEM((rows * AMP, *tile), jnp.bfloat16),
            pltpu.VMEM(integrals.shape, jnp.bfloat16),
            pltpu.VMEM(integrals.shape, jnp.bfloat16),
            pltpu.VMEM((COLS, *tile), jnp.float32),
            pltpu.VMEM((COLS, *tile), jnp.bfloat16),
            pltpu.VMEM((COLS, *tile), jnp.bfloat16),
            pltpu.VMEM((COLS, *tile), jnp.bfloat16),
            pltpu.VMEM((COLS, *tile), jnp.bfloat16),
            pltpu.VMEM((COLS, *tile), jnp.bfloat16),
            pltpu.VMEM((COLS, 2, 8, edge), jnp.int32),
            pltpu.VMEM((COLS, 2, 8, edge), jnp.int32),
            pltpu.SMEM((COLS,), jnp.int32),
            pltpu.SMEM((COLS,), jnp.int32),
            pltpu.SMEM((COLS,), jnp.int32),
            dma((CHUNKS + 6,)),
            dma((3,)), dma((3,)),
            dma((half,)), dma((half,)),
            dma((half, 3)), dma((half, 3)),
            dma((forwards,)), dma((forwards,)),
            dma((COLS,)), dma((COLS,)),
            dma((COLS,)), dma((COLS,)),
            dma((COLS,)), dma((COLS,)),
            dma((COLS,)), dma((COLS,)),
            pltpu.VMEM((OWN, *tile), jnp.float32), dma(()),
        ],
        compiler_params=pltpu.CompilerParams(collective_id=0, has_side_effects=True, vmem_limit_bytes=24 << 20),
    )(
        *(
            pltpu.with_memory_space_constraint(v, pltpu.HBM)
            for v in (amp_index, left_index, right_index, dest_col.reshape(-1), owner_slot, amplitudes, integrals)
        )
    )


def solution(mesh):
    placed = (
        P(("row", "col"), None, None),
        P(("layer", "row", "col"), None, None),
        P(("layer", "row", "col"), None),
        P(("layer", "row", "col"), None),
        P(("layer", "row", "col"), None),
        P(("row", "col"), None),
        P(("row", "col")),
    )
    return jax.shard_map(
        shards, mesh=mesh, in_specs=placed, out_specs=P(("row", "col"), None, None), check_vma=False
    )
```

```python
import jax
import jax.numpy as jnp
from jax import lax
from jax.experimental import pallas as pl
from jax.experimental.pallas import tpu as pltpu
from jax.sharding import PartitionSpec as P

MESH = pl.DeviceIdType.MESH
OWN = 8
AMP = 4
X, Y, ZLO = 4, 4, 4
COLS = X * ZLO
EARLY = COLS // 2
SELF = COLS - 1
CHUNKS = 4


def product(left, right):
    return jnp.dot(left, right, preferred_element_type=jnp.float32)


def flip(bit):
    return 1 - bit


def other_half(row, far):
    return lax.rem(row + far * Y, 2 * Y)


def next_y(row, step):
    return (row // Y) * Y + lax.rem(row + step, Y)


def destination(col, place):
    x, z = col // ZLO, col % ZLO
    half, swap, dx = flip(place // EARLY), flip((place % EARLY) // X), (place + 1) % X
    z = lax.rem(z + 2 * half, ZLO)
    z = z + swap * (1 - 2 * (z % 2))
    return lax.rem(x + dx, X) * ZLO + z


def kernel(amp_in, left_in, right_in, dest_in, slot_in, amp_hbm, int_hbm, result_ref,
           amp_ix, left_ix, right_ix, dest, slot, amps, ints, turned, part, stage_s, stage_i, got_s, got_i, got_f, tags, tags_in,
           order, first, count,
           local_sem, y_send, y_recv, z_send, z_recv, zy_send, zy_recv, f_send, f_recv,
           s_send, s_recv, i_send, i_recv, b_send, b_recv, t_send, t_recv, out, out_sem):
    layer, row, col = lax.axis_index("layer"), lax.axis_index("row"), lax.axis_index("col")
    slots, terms = amp_ix.shape
    tiles = int_hbm.shape[0]
    edge = int_hbm.shape[1]
    half = AMP // 2
    mine = half * layer
    mate = {"layer": flip(layer)}
    far = other_half(row, 1)

    barrier = pltpu.get_barrier_semaphore()
    peers = [{"row": far}, mate]
    peers += [{"row": next_y(row, s)} for s in range(1, Y)]
    for peer in peers:
        pl.semaphore_signal(barrier, inc=1, device_id=peer, device_id_type=MESH)
    for place in range(COLS):
        if place != SELF:
            pl.semaphore_signal(barrier, inc=1, device_id={"col": destination(col, place)}, device_id_type=MESH)

    own_amp = pltpu.make_async_copy(amp_hbm, amps.at[pl.ds(row * AMP, AMP)], local_sem.at[CHUNKS])
    own_amp.start()
    tables = []
    for n, (src, dst) in enumerate(
        ((dest_in, dest), (slot_in, slot), (amp_in, amp_ix), (left_in, left_ix), (right_in, right_ix))
    ):
        tables.append(pltpu.make_async_copy(src, dst, local_sem.at[CHUNKS + 1 + n]))
        tables[-1].start()
    loads = []
    step = tiles // CHUNKS
    for c in range(CHUNKS):
        loads.append(pltpu.make_async_copy(int_hbm.at[pl.ds(c * step, step)], ints.at[pl.ds(c * step, step)], local_sem.at[c]))
        loads[-1].start()

    def turn(c):
        loads[c].wait()

        def four(i, _):
            for j in range(4):
                turned[c * step + 4 * i + j] = ints[c * step + 4 * i + j].T
            return 0

        lax.fori_loop(0, step // 4, four, 0)

    own_amp.wait()
    pl.semaphore_wait(barrier, len(peers) + COLS - 1)

    def block(r, n=half, at=0):
        return amps.at[pl.ds(r * AMP + mine + at, n)]

    def send(src, dst, out_sem, in_sem, peer):
        return pltpu.make_async_remote_copy(
            src_ref=src, dst_ref=dst, send_sem=out_sem, recv_sem=in_sem, device_id=peer, device_id_type=MESH
        )

    z_copies = [send(block(row, 1, t), block(row, 1, t), z_send.at[t], z_recv.at[t], {"row": far}) for t in range(half)]
    for c in z_copies:
        c.start()
    y_copies = [
        send(block(row), block(row), y_send.at[s - 1], y_recv.at[s - 1], {"row": next_y(row, s)}) for s in (1, 3, 2)
    ]
    for c in y_copies:
        c.start()
    x, z = col // ZLO, col % ZLO

    def place_of(k):
        to = dest[k]
        dx = lax.rem(to // ZLO - x + 2 * X - 1, X)
        zt = lax.rem(to, ZLO)
        same = jnp.where(zt // 2 == z // 2, 1, 0)
        even = jnp.where(zt % 2 == z % 2, 1, 0)
        return same * EARLY + even * X + dx

    for c in tables:
        c.wait()
    places = [place_of(k) for k in range(slots)]
    ranks = []
    for k in range(slots):
        rank = 0
        for j in range(slots):
            if j < k:
                rank = rank + jnp.where(places[j] <= places[k], 1, 0)
            elif j > k:
                rank = rank + jnp.where(places[j] < places[k], 1, 0)
        ranks.append(rank)
    for i in range(slots):
        at, below, same = 0, 0, 0
        for k in range(slots):
            at = at + jnp.where(ranks[k] == i, k, 0)
            below = below + jnp.where(places[k] < i, 1, 0)
            same = same + jnp.where(places[k] == i, 1, 0)
        order[i] = at
        first[i] = below
        count[i] = same

    for c in range(2):
        turn(c)
    to_mate = []

    def forward(r, n, at, k):
        to_mate.append(send(block(r, n, at), block(r, n, at), f_send.at[k], f_recv.at[k], mate))
        to_mate[-1].start()

    def arrived(r, n, at, sem):
        send(block(r, n, at), block(r, n, at), f_send.at[0], sem, mate).wait_recv()

    came = []

    def take(r, n, at, sem):
        arrived(r, n, at, sem)
        forward(r, n, at, len(came))
        came.append((r, n, at, len(came)))

    zy_copies = []
    for t in range(half):
        arrived(far, 1, t, z_recv.at[t])
        for s in (2, 1, 3):
            zy_copies.append(send(block(far, 1, t), block(far, 1, t), zy_send.at[t, s - 1], zy_recv.at[t, s - 1],
                                  {"row": next_y(row, s)}))
            zy_copies[-1].start()
        forward(far, 1, t, len(came))
        came.append((far, 1, t, len(came)))
    for s in (1, 3, 2):
        take(next_y(row, Y - s), half, 0, y_recv.at[s - 1])
    for c in range(2, CHUNKS):
        turn(c)

    def pick(place, j):
        at = jnp.minimum(first[place] + j, slots - 1)
        return at, j < count[place]

    def tag(place, _):
        for j in range(2):
            at, there = pick(place, j)
            tags[place, j] = jnp.full((8, edge), jnp.where(there, slot[order[at]], OWN), jnp.int32)
        return 0

    lax.fori_loop(0, COLS, tag, 0)

    tag_copies = []
    for place in range(COLS):
        if place != SELF:
            tag_copies.append(send(tags.at[place], tags_in.at[place], t_send.at[place], t_recv.at[place],
                                   {"col": destination(col, place)}))
            tag_copies[-1].start()

    for t in range(half):
        for s in (1, 3, 2):
            take(next_y(far, Y - s), 1, t, zy_recv.at[t, s - 1])

    def of_mate(r, n, at):
        return amps.at[pl.ds(r * AMP + half * flip(layer) + at, n)]

    for r, n, at, k in came:
        send(of_mate(r, n, at), of_mate(r, n, at), f_send.at[0], f_recv.at[k], mate).wait_recv()

    def s_copy(p):
        return send(stage_s.at[p], got_s.at[p], s_send.at[p], s_recv.at[p], mate)

    def i_copy(p):
        return send(stage_i.at[p], got_i.at[p], i_send.at[p], i_recv.at[p], {"col": destination(col, p)})

    def b_copy(p):
        return send(got_i.at[p], got_f.at[p], b_send.at[p], b_recv.at[p], mate)

    def chosen(p, j):
        at, there = pick(p, j)
        return part[at] * jnp.where(there, 1.0, 0.0)

    def add_sibling(i):
        part[i] += got_s[i].astype(jnp.float32)

    def stage_owner(p):
        stage_i[p] = chosen(p, layer).astype(jnp.bfloat16)

    def to_owner(p):
        stage_owner(p)
        i_copy(p).start()

    def result(i):
        k = order[i]
        middles, lefts = [], []
        for t in range(terms):
            middles.append(product(amps[amp_ix[k, t]], turned[right_ix[k, t]]).astype(jnp.bfloat16))
            lefts.append(ints[left_ix[k, t]])
        part[i] = product(jnp.concatenate(lefts, 1), jnp.concatenate(middles, 0))

    def two(i):
        for k in (2 * i, 2 * i + 1):
            result(k)
        for k in (2 * i, 2 * i + 1):
            stage_s[k] = part[k].astype(jnp.bfloat16)

    def start_two(i):
        for k in (2 * i, 2 * i + 1):
            s_copy(k).start()

    def opening(i, _):
        two(i)
        start_two(i)
        return 0

    def steady(i, _):
        for k in (2 * i - 4, 2 * i - 3):
            s_copy(k).wait_recv()
        for k in (2 * i - 4, 2 * i - 3):
            add_sibling(k)
        to_owner(i - 2)
        two(i)
        start_two(i)
        return 0

    lax.fori_loop(0, 2, opening, 0)
    lax.fori_loop(2, slots // 2, steady, 0)
    for k in (slots - 4, slots - 3):
        s_copy(k).wait_recv()
        add_sibling(k)
    to_owner(EARLY - 2)
    def onward(p, _):
        i_copy(p).wait_recv()
        b_copy(p).start()
        return 0

    lax.fori_loop(0, EARLY - 3, onward, 0)
    for k in (slots - 2, slots - 1):
        s_copy(k).wait_recv()
        add_sibling(k)
    to_owner(EARLY - 1)

    def rest(p, _):
        to_owner(p)
        return 0

    lax.fori_loop(EARLY, SELF, rest, 0)
    got_i[SELF] = chosen(SELF, layer).astype(jnp.bfloat16)
    b_copy(SELF).start()
    for place in range(COLS):
        if place != SELF:
            send(tags.at[place], tags_in.at[place], t_send.at[place], t_recv.at[place], mate).wait_recv()
    tags_in[SELF] = tags[SELF]

    def add(p, ref, j):
        label = tags_in[p, j]
        tile = ref[p].astype(jnp.float32).reshape(edge // 8, 8, edge)
        for s in range(OWN):
            there = jnp.where(label == s, 1.0, 0.0)
            out[s] += (tile * there[None]).reshape(edge, edge)

    def onward_add(p, _):
        onward(p, 0)
        add(p, got_i, layer)
        return 0

    def add_own(p, _):
        add(p, got_i, layer)
        return 0

    def add_mate(p, _):
        b_copy(p).wait_recv()
        add(p, got_f, flip(layer))
        return 0

    lax.fori_loop(EARLY - 3, EARLY - 1, onward, 0)
    out[...] = jnp.zeros_like(out)
    add_own(SELF, 0)
    lax.fori_loop(0, EARLY - 1, add_own, 0)
    add_mate(SELF, 0)
    lax.fori_loop(0, EARLY - 1, add_mate, 0)
    lax.fori_loop(EARLY - 1, SELF, onward_add, 0)
    lax.fori_loop(EARLY - 1, SELF, add_mate, 0)

    final = pltpu.make_async_copy(out, result_ref, out_sem)
    final.start()

    def drain(p, _):
        s_copy(p).wait_send()
        b_copy(p).wait_send()
        return 0

    lax.fori_loop(0, COLS, drain, 0)
    for c in z_copies + y_copies + zy_copies + to_mate:
        c.wait_send()
    for place in range(COLS):
        if place != SELF:
            i_copy(place).wait_send()
    for c in tag_copies:
        c.wait_send()
    final.wait()


def shards(amplitudes, integrals, amp_index, left_index, right_index, dest_col, owner_slot):
    edge = integrals.shape[1]
    half = AMP // 2
    rows = lax.axis_size("row")
    tile = (edge, edge)
    dma = pltpu.SemaphoreType.DMA
    in_hbm = pl.BlockSpec(memory_space=pl.ANY)
    forwards = 3 + half + 3 * half
    return pl.pallas_call(
        kernel,
        out_shape=jax.ShapeDtypeStruct((OWN, *tile), jnp.float32),
        in_specs=[in_hbm] * 7,
        out_specs=pl.BlockSpec(memory_space=pl.ANY),
        scratch_shapes=[
            pltpu.SMEM(amp_index.shape, jnp.int32),
            pltpu.SMEM(left_index.shape, jnp.int32),
            pltpu.SMEM(right_index.shape, jnp.int32),
            pltpu.SMEM((COLS,), jnp.int32),
            pltpu.SMEM((COLS,), jnp.int32),
            pltpu.VMEM((rows * AMP, *tile), jnp.bfloat16),
            pltpu.VMEM(integrals.shape, jnp.bfloat16),
            pltpu.VMEM(integrals.shape, jnp.bfloat16),
            pltpu.VMEM((COLS, *tile), jnp.float32),
            pltpu.VMEM((COLS, *tile), jnp.bfloat16),
            pltpu.VMEM((COLS, *tile), jnp.bfloat16),
            pltpu.VMEM((COLS, *tile), jnp.bfloat16),
            pltpu.VMEM((COLS, *tile), jnp.bfloat16),
            pltpu.VMEM((COLS, *tile), jnp.bfloat16),
            pltpu.VMEM((COLS, 2, 8, edge), jnp.int32),
            pltpu.VMEM((COLS, 2, 8, edge), jnp.int32),
            pltpu.SMEM((COLS,), jnp.int32),
            pltpu.SMEM((COLS,), jnp.int32),
            pltpu.SMEM((COLS,), jnp.int32),
            dma((CHUNKS + 6,)),
            dma((3,)), dma((3,)),
            dma((half,)), dma((half,)),
            dma((half, 3)), dma((half, 3)),
            dma((forwards,)), dma((forwards,)),
            dma((COLS,)), dma((COLS,)),
            dma((COLS,)), dma((COLS,)),
            dma((COLS,)), dma((COLS,)),
            dma((COLS,)), dma((COLS,)),
            pltpu.VMEM((OWN, *tile), jnp.float32), dma(()),
        ],
        compiler_params=pltpu.CompilerParams(collective_id=0, has_side_effects=True, vmem_limit_bytes=24 << 20),
    )(
        *(
            pltpu.with_memory_space_constraint(v, pltpu.HBM)
            for v in (amp_index, left_index, right_index, dest_col.reshape(-1), owner_slot, amplitudes, integrals)
        )
    )


def solution(mesh):
    placed = (
        P(("row", "col"), None, None),
        P(("layer", "row", "col"), None, None),
        P(("layer", "row", "col"), None),
        P(("layer", "row", "col"), None),
        P(("layer", "row", "col"), None),
        P(("row", "col"), None),
        P(("row", "col")),
    )
    return jax.shard_map(
        shards, mesh=mesh, in_specs=placed, out_specs=P(("row", "col"), None, None), check_vma=False
    )
```
